32 devices in a mesh: row: 4 (over y, x), col: 8 (over z, core).
Axes of the slice: x: 2, y: 2, z: 4, core: 2. Of those that a mesh axis runs over, the one named last changes fastest.
Arguments:
- inverse: float32 [20480, 20480], P('row', 'col'), may hold values from -1 to 3
- panels: float32 [3, 1024, 512], P(None, 'col'), may hold values from -0.375 to 0.375
- blocks: int32 [3, 8], replicated, may hold values from 0 to 159, as said below
- diag_inverse: float32 [3, 512, 512], replicated, may hold values from -6 to 6
Outputs:
- update: float32 [3, 20480, 512], P(None, ('row', 'col'))
- diag_out: float32 [3, 512, 512], replicated
The draws below stay inside these ranges and needn't reach their ends.
Inputs may be any that keep to these rules, and one draw needn't show every extreme that they name: `blocks`: each row holds 8 different block numbers in increasing order.
All inputs are finite; a program needn't handle non-finite values.
Results may differ from the reference program's by a relative error of at most 0.0001.
Values sent between devices are 32-bit elements; how exact they have to be, the bound alone decides.
No kernel may reach another device: no remote copies, remote signals or barrier semaphores. Data moves between devices by JAX's collectives and lax.ppermute only.
A program may use at most 192 MiB of HBM per device.

```python
import jax
import jax.numpy as jnp
from jax import lax

NA = 20480
W = 512
BLK = 128
SIB = 3
NBP = 8


def draw_inverse(key, part):
    base = jax.random.normal(key, (NA, NA), jnp.float32)
    symmetric = (base + base.T) * (0.99 / jnp.sqrt(jnp.float32(NA)))
    diagonal = jax.random.uniform(jax.random.fold_in(key, 11), (NA,), jnp.float32, 1.0, 2.0)
    return symmetric + jnp.diag(diagonal)


def draw_blocks(key, part):
    listed = []
    for sibling in range(SIB):
        order = jax.random.permutation(jax.random.fold_in(key, sibling + 7), NA // BLK)
        listed.append(jnp.sort(order[:NBP]))
    return jnp.stack(listed).astype(jnp.int32)


def shard_levels(stream_key, shape, cuts, least, top_value):
    def one(position, shards_of):
        heights = jax.random.uniform(jax.random.fold_in(jax.random.fold_in(stream_key, 6), position), (shards_of,), jnp.float32, least / len(cuts), top_value / len(cuts))
        return jnp.repeat(jnp.exp(heights), shape[position] // shards_of).reshape((-1,) + (1,) * (len(shape) - position - 1))

    gain = one(*cuts[0])
    for cut in cuts[1:]:
        gain = gain * one(*cut)
    return gain


def normal_values(rng, dims, deviation, reach, cuts=(), kind=jnp.bfloat16):
    level = shard_levels(rng, dims, cuts, -0.22, 0.18) if cuts else 1.0
    entries = jax.random.normal(rng, dims, jnp.float32) * deviation * level
    return jnp.minimum(jnp.maximum(entries, -reach), reach).astype(kind)


def setup_inputs(seed: int = 0) -> dict:
    splits = jax.random.split(jax.random.key(seed), 5)
    return {
        "inverse": draw_inverse(jax.random.fold_in(splits[4], 71), 0),
        "panels": normal_values(splits[1], (SIB, NBP * BLK, W), (NBP * BLK // 4) ** -0.5, 0.375, ((1, 8),), jnp.float32),
        "blocks": draw_blocks(jax.random.fold_in(splits[4], 71), 0),
        "diag_inverse": normal_values(splits[3], (SIB, W, W), 1.0, 6.0, (), jnp.float32),
    }


def reference(inverse, panels, blocks, diag_inverse):
    offsets = (blocks[:, :, None] * BLK + jnp.arange(BLK, dtype=jnp.int32)[None, None, :]).reshape(SIB, NBP * BLK).astype(jnp.int32)
    updates = []
    diagonals = []
    for sibling in range(SIB):
        expanded = jnp.zeros((NA, W), jnp.float32).at[offsets[sibling]].set(panels[sibling])
        update = -jnp.dot(inverse, expanded, precision=lax.Precision.HIGHEST, preferred_element_type=jnp.float32)
        updates.append(update)
        diagonals.append(diag_inverse[sibling] + jnp.dot(expanded.T, update, precision=lax.Precision.HIGHEST, preferred_element_type=jnp.float32))
    return jnp.stack(updates), jnp.stack(diagonals)
```

```python
import functools

import jax
import jax.numpy as jnp
from jax import lax
from jax.experimental import pallas as pl
from jax.experimental.pallas import tpu as pltpu
from jax.sharding import PartitionSpec as P


BLK = 128


def split(x):
    hi = x.astype(jnp.bfloat16)
    return hi, (x - hi.astype(jnp.float32)).astype(jnp.bfloat16)


def upper(i, j, n):
    return i * n - i * (i - 1) // 2 + j - i


def place(q, order):
    slot = 0
    for bit in order:
        slot = slot * 2 + (q // bit) % 2
    return slot


def product_kernel(rows, half_of, ids, inv, pan, *refs):
    outs, (diag_out, acc, diag, buf, in_sem, out_sem) = refs[:-6], refs[-6:]
    nbp = pan.shape[0] // BLK
    cols, width = acc.shape
    row_rank, col_rank = lax.axis_index("row"), lax.axis_index("col")
    row_blocks, col_blocks = inv.shape[0] // BLK, cols // BLK

    def below(limit):
        count = jnp.int32(0)
        for b in range(nbp):
            count += (ids[b] < limit).astype(jnp.int32)
        return count

    first, last = below(row_rank * row_blocks), below((row_rank + 1) * row_blocks)

    def fetch(b):
        row = pl.multiple_of((ids[b] - row_rank * row_blocks) * BLK, BLK)
        return pltpu.make_async_copy(inv.at[pl.ds(row, BLK), :], buf.at[b % 2], in_sem.at[b % 2])

    @pl.when(first < last)
    def _():
        fetch(first).start()

    acc[...] = jnp.zeros_like(acc)
    diag[...] = jnp.zeros_like(diag)

    @pl.loop(first, last)
    def _(b):
        @pl.when(b + 1 < last)
        def _():
            fetch(b + 1).start()

        hi, lo = split(pan[pl.ds(pl.multiple_of(b * BLK, BLK), BLK), :])
        right = jnp.concatenate([hi, lo, hi], axis=0)
        fetch(b).wait()
        for u in range(cols // BLK):
            at = slice(u * BLK, (u + 1) * BLK)
            hi, lo = split(jnp.transpose(buf[b % 2, :, at]))
            left = jnp.concatenate([hi, hi, lo], axis=1)
            acc[at, :] -= jnp.dot(left, right, preferred_element_type=jnp.float32)

    copies = []
    for half, order, flip, send, keep in half_of(outs):
        lanes = slice(half * width // 2, (half + 1) * width // 2)
        pieces = cols // rows
        for t in range(pieces):
            slot = place(jnp.bitwise_xor(row_rank, t ^ flip), order)
            src = acc.at[pl.ds(t * rows, rows), lanes]
            sem = out_sem.at[half * pieces + t]

            @pl.when(slot < pieces // 2)
            def _(src=src, sem=sem, slot=slot, keep=keep):
                pltpu.make_async_copy(src, keep.at[slot], sem).start()

            @pl.when(slot >= pieces // 2)
            def _(src=src, sem=sem, slot=slot, send=send):
                pltpu.make_async_copy(src, send.at[slot - pieces // 2], sem).start()

            copies.append(pltpu.make_async_copy(src, keep.at[0], sem))

    first, last = below(col_rank * col_blocks), below((col_rank + 1) * col_blocks)

    @pl.loop(first, last)
    def _(b):
        hi, lo = split(jnp.transpose(pan[pl.ds(pl.multiple_of(b * BLK, BLK), BLK), :]))
        left = jnp.concatenate([hi, hi, lo], axis=1)
        row = pl.multiple_of((ids[b] - col_rank * col_blocks) * BLK, BLK)
        hi, lo = split(acc[pl.ds(row, BLK), :])
        right = jnp.concatenate([hi, lo, hi], axis=0)
        for i in range(width // BLK):
            at = slice(i * BLK, (i + 1) * BLK)
            strip = jnp.dot(left[at, :], right[:, i * BLK :], preferred_element_type=jnp.float32)
            for j in range(i, width // BLK):
                at = slice((j - i) * BLK, (j - i + 1) * BLK)
                diag[upper(i, j, width // BLK)] += strip[:, at]

    out = pltpu.make_async_copy(diag, diag_out, out_sem.at[len(copies)])
    out.start()
    for copy in copies:
        copy.wait()
    out.wait()


def product(rows, orders, ids, inverse, panel):
    cols, width = inverse.shape[1], panel.shape[1]
    pieces = cols // rows
    part = jax.ShapeDtypeStruct((pieces // 2, rows, width // 2), jnp.float32)
    flops = 6 * cols * width * BLK * 2

    def half_of(outs):
        return [(h, orders[h][0], orders[h][1], outs[2 * h], outs[2 * h + 1]) for h in range(2)]

    n = width // BLK
    packed = (n * (n + 1) // 2, BLK, BLK)
    anywhere = pl.BlockSpec(memory_space=pl.ANY)
    in_hbm = pl.BlockSpec(memory_space=pltpu.HBM)
    return pl.pallas_call(
        functools.partial(product_kernel, rows, half_of),
        out_shape=(part,) * 4 + (jax.ShapeDtypeStruct(packed, jnp.float32),),
        in_specs=[
            pl.BlockSpec(memory_space=pltpu.SMEM),
            anywhere,
            pl.BlockSpec(memory_space=pltpu.VMEM),
        ],
        out_specs=(in_hbm,) * 5,
        scratch_shapes=[
            pltpu.VMEM((cols, width), jnp.float32),
            pltpu.VMEM(packed, jnp.float32),
            pltpu.VMEM((2, BLK, cols), jnp.float32),
            pltpu.SemaphoreType.DMA((2,)),
            pltpu.SemaphoreType.DMA((2 * pieces + 1,)),
        ],
        compiler_params=pltpu.CompilerParams(vmem_limit_bytes=16 << 20),
        cost_estimate=pl.CostEstimate(flops=flops, bytes_accessed=8 * cols * width, transcendentals=0),
    )(ids, inverse, panel)


def mirror_kernel(total, old, out):
    n = out.shape[1] // BLK
    for i in range(n):
        for j in range(i, n):
            block = total[0, upper(i, j, n)]
            rows, cols = slice(i * BLK, (i + 1) * BLK), slice(j * BLK, (j + 1) * BLK)
            out[0, rows, cols] = old[0, rows, cols] + block
            if i < j:
                out[0, cols, rows] = old[0, cols, rows] + jnp.transpose(block)


def mirror(total, old):
    one = lambda x: pl.BlockSpec((1,) + x.shape[1:], lambda s: (s,) + (0,) * (x.ndim - 1))
    return pl.pallas_call(
        mirror_kernel,
        grid=(old.shape[0],),
        out_shape=jax.ShapeDtypeStruct(old.shape, old.dtype),
        in_specs=[one(total), one(old)],
        out_specs=one(old),
    )(total, old)


def on_any_mesh(row_devices, col_devices, inverse, panels, blocks, diag_inverse):
    siblings, _, _ = panels.shape
    rows = inverse.shape[0] // col_devices
    bits = [1 << i for i in range(row_devices.bit_length() - 1)]
    orders = ((bits, 0), (bits[::-1], row_devices // 2))

    def swap(x, bit):
        pairs = [
            (r * col_devices + c, (r ^ bit) * col_devices + c)
            for r in range(row_devices)
            for c in range(col_devices)
        ]
        return lax.ppermute(x, ("row", "col"), pairs)

    def deliver(x, flip):
        pairs = [
            (r * col_devices + c, c * row_devices + (r ^ flip))
            for r in range(row_devices)
            for c in range(col_devices)
        ]
        return lax.ppermute(x, ("row", "col"), pairs)

    first = lax.all_gather(panels[0], "col", axis=0, tiled=True)
    rest = lax.all_gather(panels[1:], "col", axis=1, tiled=True)
    updates, diags = [], []
    for s in range(siblings):
        panel = first if s == 0 else rest[s - 1]
        *parts, diag = product(rows, orders, blocks[s], inverse, panel)
        diags.append(diag)
        halves = []
        for h, (order, flip) in enumerate(orders):
            send, keep = parts[2 * h], parts[2 * h + 1]
            for bit in order:
                got = swap(send, bit)
                n = keep.shape[0] // 2
                if n:
                    send, keep = keep[n:] + got[n:], keep[:n] + got[:n]
                    if s == 0:
                        rest, send = lax.optimization_barrier((rest, send))
                else:
                    keep = keep + got
            halves.append(deliver(keep[0], flip))
        updates.append(jnp.concatenate(halves, axis=1))
    diag_total = lax.psum(jnp.stack(diags), ("row", "col"))
    return jnp.stack(updates), mirror(diag_total, diag_inverse)


def below(ids, count, limit):
    total = jnp.int32(0)
    for b in range(count):
        total += (ids[b] < limit).astype(jnp.int32)
    return total


def panel_block(own, other, b):
    row, col = lax.axis_index("row"), lax.axis_index("col")
    near = jnp.bitwise_xor(b // 2, col // 2)
    mine = b % 2 == col % 2
    if len(own.shape) == 3:
        return jnp.where(mine, own[near], other[near])
    parts = []
    for r in range(own.shape[0]):
        at = jnp.bitwise_xor(row, r)
        parts.append(jnp.where(mine, own[at, near], other[at, near]))
    return jnp.concatenate(parts, axis=0)


def picked_rows_kernel(sending, cuts, ids, inv, own, other, *refs):
    outs, (diag_out, acc, diag, buf, in_sem, out_sem) = refs[:-6], refs[-6:]
    count, (cols, width) = ids.shape[0], acc.shape
    k, col = lax.axis_index("row"), lax.axis_index("col")
    row_blocks, col_blocks = inv.shape[0] // BLK, cols // BLK
    first, last = below(ids, count, k * row_blocks), below(ids, count, (k + 1) * row_blocks)
    turn = (col % 2 != k // 2).astype(jnp.int32)
    chunk = jnp.bitwise_xor(k % 2, 1 - turn if sending else turn)

    def fetch(b):
        row = pl.multiple_of((ids[b] - k * row_blocks) * BLK, BLK)
        src = inv.at[pl.ds(row, BLK), pl.ds(pl.multiple_of(chunk * cols, BLK), cols)]
        return pltpu.make_async_copy(src, buf.at[b % 2], in_sem.at[b % 2])

    @pl.when(first < last)
    def _():
        fetch(first).start()

    acc[...] = jnp.zeros_like(acc)
    diag[...] = jnp.zeros_like(diag)

    @pl.loop(first, last)
    def _(b):
        @pl.when(b + 1 < last)
        def _():
            fetch(b + 1).start()

        hi, lo = split(panel_block(own, other, b))
        right = jnp.concatenate([hi, lo, hi], axis=0)
        fetch(b).wait()
        for u in range(cols // BLK):
            at = slice(u * BLK, (u + 1) * BLK)
            hi, lo = split(jnp.transpose(buf[b % 2, :, at]))
            left = jnp.concatenate([hi, hi, lo], axis=1)
            acc[at, :] -= jnp.dot(left, right, preferred_element_type=jnp.float32)

    half = cols // 2
    n0, n1 = cuts
    copies = []

    def put(row, size, dst):
        src = acc.at[pl.ds(pl.multiple_of(row, 8), size), :]
        copies.append(pltpu.make_async_copy(src, dst, out_sem.at[len(copies)]))

    for u in range(2):
        row = u * half
        if sending:
            first_send, kept = outs
            put(row, n0, first_send.at[u, pl.ds(0, n0)])
            put(row + n0 + (1 - turn) * n1, n1, first_send.at[jnp.bitwise_xor(u, 1 - turn), pl.ds(n0, n1)])
            put(row + n0 + turn * n1, n1, kept.at[jnp.bitwise_xor(u, turn)])
        else:
            base0, base1, base2 = outs
            put(row, n0, base0.at[u])
            put(row + n0, n1, base1.at[u])
            put(row + n0 + n1, n1, base2.at[1 - u])
    for copy in copies:
        copy.start()

    start = (col * 2 + chunk) * col_blocks
    first, last = below(ids, count, start), below(ids, count, start + col_blocks)

    @pl.loop(first, last)
    def _(b):
        hi, lo = split(jnp.transpose(panel_block(own, other, b)))
        left = jnp.concatenate([hi, hi, lo], axis=1)
        row = pl.multiple_of((ids[b] - start) * BLK, BLK)
        hi, lo = split(acc[pl.ds(row, BLK), :])
        right = jnp.concatenate([hi, lo, hi], axis=0)
        for i in range(width // BLK):
            at = slice(i * BLK, (i + 1) * BLK)
            strip = jnp.dot(left[at, :], right[:, i * BLK :], preferred_element_type=jnp.float32)
            for j in range(i, width // BLK):
                at = slice((j - i) * BLK, (j - i + 1) * BLK)
                diag[upper(i, j, width // BLK)] += strip[:, at]

    out = pltpu.make_async_copy(diag, diag_out, out_sem.at[len(copies)])
    out.start()
    for copy in copies:
        copy.wait()
    out.wait()


def picked_rows(sending, cuts, ids, inverse, own, other, width):
    cols = inverse.shape[1] // 2
    n = width // BLK
    n0, n1 = cuts
    f32 = jnp.float32
    packed = (n * (n + 1) // 2, BLK, BLK)
    shapes = [(2, n0 + n1, width), (2, n1, width)] if sending else [(2, n, width) for n in (n0, n1, n1)]
    shapes.append(packed)
    in_hbm = pl.BlockSpec(memory_space=pltpu.HBM)
    in_vmem = pl.BlockSpec(memory_space=pltpu.VMEM)
    return pl.pallas_call(
        functools.partial(picked_rows_kernel, sending, cuts),
        out_shape=tuple(jax.ShapeDtypeStruct(x, f32) for x in shapes),
        in_specs=[pl.BlockSpec(memory_space=pltpu.SMEM), pl.BlockSpec(memory_space=pl.ANY), in_vmem, in_vmem],
        out_specs=(in_hbm,) * len(shapes),
        scratch_shapes=[
            pltpu.VMEM((cols, width), f32),
            pltpu.VMEM(packed, f32),
            pltpu.VMEM((2, BLK, cols), f32),
            pltpu.SemaphoreType.DMA((2,)),
            pltpu.SemaphoreType.DMA((7,)),
        ],
        compiler_params=pltpu.CompilerParams(vmem_limit_bytes=16 << 20),
        cost_estimate=pl.CostEstimate(
            flops=12 * cols * width * BLK, bytes_accessed=8 * cols * width, transcendentals=0
        ),
    )(ids, inverse, own, other)


def picked_cols_kernel(ids, inv, own, other, mine_out, send_out, acc, buf, in_sem, out_sem):
    count, (rows, width) = ids.shape[0], acc.shape
    col = lax.axis_index("col")
    col_blocks = inv.shape[1] // BLK
    first, last = below(ids, count, col * col_blocks), below(ids, count, (col + 1) * col_blocks)
    top = pl.multiple_of(col // 2 * rows, rows)

    def fetch(b):
        at = pl.multiple_of((ids[b] - col * col_blocks) * BLK, BLK)
        src = inv.at[pl.ds(top, rows), pl.ds(at, BLK)]
        return pltpu.make_async_copy(src, buf.at[b % 2], in_sem.at[b % 2])

    @pl.when(first < last)
    def _():
        fetch(first).start()

    acc[...] = jnp.zeros_like(acc)

    @pl.loop(first, last)
    def _(b):
        @pl.when(b + 1 < last)
        def _():
            fetch(b + 1).start()

        hi, lo = split(panel_block(own, other, b))
        right = jnp.concatenate([hi, lo, hi], axis=0)
        fetch(b).wait()
        for u in range(rows // BLK):
            at = slice(u * BLK, (u + 1) * BLK)
            hi, lo = split(buf[b % 2, at, :])
            left = jnp.concatenate([hi, hi, lo], axis=1)
            acc[at, :] -= jnp.dot(left, right, preferred_element_type=jnp.float32)

    half = rows // 2
    copies = []
    for i, out in enumerate((mine_out, send_out)):
        at = pl.multiple_of(jnp.bitwise_xor(col % 2, i) * half, half)
        copies.append(pltpu.make_async_copy(acc.at[pl.ds(at, half), :], out, out_sem.at[i]))
    for copy in copies:
        copy.start()
    for copy in copies:
        copy.wait()


def picked_cols(ids, inverse, own, other, rows, width):
    f32 = jnp.float32
    part = jax.ShapeDtypeStruct((rows // 2, width), f32)
    in_hbm = pl.BlockSpec(memory_space=pltpu.HBM)
    in_vmem = pl.BlockSpec(memory_space=pltpu.VMEM)
    return pl.pallas_call(
        picked_cols_kernel,
        out_shape=(part, part),
        in_specs=[pl.BlockSpec(memory_space=pltpu.SMEM), pl.BlockSpec(memory_space=pl.ANY), in_vmem, in_vmem],
        out_specs=(in_hbm, in_hbm),
        scratch_shapes=[
            pltpu.VMEM((rows, width), f32),
            pltpu.VMEM((2, rows, BLK), f32),
            pltpu.SemaphoreType.DMA((2,)),
            pltpu.SemaphoreType.DMA((2,)),
        ],
        compiler_params=pltpu.CompilerParams(vmem_limit_bytes=16 << 20),
        cost_estimate=pl.CostEstimate(
            flops=6 * rows * width * BLK, bytes_accessed=8 * rows * width, transcendentals=0
        ),
    )(ids, inverse, own, other)


def on_planes(R, C, inverse, panels, blocks, diag_inverse):
    siblings, share, width = panels.shape
    rows = inverse.shape[0] // C
    Z = C // 2
    n1 = rows // 32 * 8
    cuts = (rows - 2 * n1, n1)
    row, col = lax.axis_index("row"), lax.axis_index("col")
    core, chip = col % 2, col // 2

    def permute(x, target):
        pairs = []
        for r in range(R):
            for c in range(C):
                to = target(r, c)
                if to is not None:
                    pairs.append((r * C + c, to[0] * C + to[1]))
        return lax.ppermute(x, ("row", "col"), pairs)

    def hop(x, dr, dc):
        return permute(x, lambda r, c: (r ^ dr, c ^ dc))

    def turned(r, c):
        return c % 2 != r // 2

    def take(x, i):
        return lax.dynamic_index_in_dim(x, i, 0, keepdims=False)

    quarter = take(panels[0].reshape(R, share // R, width), row)
    early = [quarter] + [hop(quarter, 0, 2 * d) for d in range(1, Z)]
    early = jnp.stack(early)
    early = jnp.stack([early] + [hop(early, d, 0) for d in range(1, R)])
    gathered = [(early, hop(early, 0, 1))]
    for s in range(1, siblings):
        late = jnp.stack([panels[s]] + [hop(panels[s], 0, 2 * d) for d in range(1, Z)])
        gathered.append((late, hop(late, 0, 1)))

    states, diags = [], []
    for s in range(siblings):
        send, kept, diag_a = picked_rows(True, cuts, blocks[s], inverse, *gathered[s], width)
        by_y = permute(send, lambda r, c: None if turned(r, c) else (r ^ 2, c))
        by_x = permute(send, lambda r, c: (r ^ 1, c) if turned(r, c) else None)
        base0, base1, base2, diag_b = picked_rows(False, cuts, blocks[s], inverse, *gathered[s], width)
        diags.append(diag_a + diag_b)
        n0 = cuts[0]
        to_y = base1 + by_x[:, n0:]
        to_x = base2 + by_y[:, n0:]
        final0 = base0 + by_x[:, :n0] + by_y[:, :n0]
        got_y = permute(to_y, lambda r, c: (r ^ 2, c) if turned(r, c) else None)
        got_x = permute(to_x, lambda r, c: (r ^ 1, c) if turned(r, c) else None)
        final = kept + got_y + got_x
        states.append((final0, final))

    v = jnp.stack(diags)
    shape = v.shape
    v = v.reshape(2, R, Z, -1, BLK)
    v = take(v, core) + hop(take(v, 1 - core), 0, 1)
    parts = [take(v, row)] + [hop(take(v, row ^ d), d, 0) for d in range(1, R)]
    v = functools.reduce(jnp.add, parts)
    parts = [take(v, chip)] + [hop(take(v, chip ^ d), 0, 2 * d) for d in range(1, Z)]
    v = functools.reduce(jnp.add, parts)

    def spread(x, at, n, step):
        parts = [x] + [step(x, d) for d in range(1, n)]
        out = jnp.zeros((n,) + x.shape, x.dtype)
        for d in range(n):
            out = lax.dynamic_update_index_in_dim(out, parts[d], at ^ d, 0)
        return out

    v = spread(v, chip, Z, lambda x, d: hop(x, 0, 2 * d))
    v = spread(v, row, R, lambda x, d: hop(x, d, 0))
    v = spread(v, core, 2, lambda x, d: hop(x, 0, d))
    diag_out = mirror(v.reshape(shape), diag_inverse)

    updates = []
    for s in range(siblings):
        final0, final = states[s]
        mine, theirs = picked_cols(blocks[s], inverse, *gathered[s], 2 * rows, width)
        local = mine + hop(theirs, 0, 1)
        d, e = [], []
        for u in range(2):
            d.append(permute(final0[u], lambda r, c: (c // 2, 2 * (r ^ 3) + u) if turned(r, c) else None))
            e.append(
                permute(
                    final[u], lambda r, c: (c // 2, 2 * (r ^ 2) + 1 - u) if turned(r, c) else (c // 2, 2 * (r ^ 1) + u)
                )
            )
        even = core == 0
        parts = [jnp.where(even, d[0], d[1]), jnp.where(even, e[0], e[1]), jnp.where(even, e[1], e[0])]
        updates.append(jnp.concatenate(parts, axis=0) + local)

    return jnp.stack(updates), diag_out


def fits_planes(row_devices, col_devices):
    return row_devices == 4 and col_devices == 8


def on_device(row_devices, col_devices, *args):
    planes = fits_planes(row_devices, col_devices)
    return (on_planes if planes else on_any_mesh)(row_devices, col_devices, *args)


def solution(mesh):
    sizes = mesh.shape["row"], mesh.shape["col"]
    return jax.shard_map(
        functools.partial(on_device, *sizes),
        mesh=mesh,
        in_specs=(P("row", "col"), P(None, "col", None), P(), P()),
        out_specs=(P(None, ("row", "col"), None), P()),
        check_vma=False,
    )
```
